128 devices in a mesh: grp: 4 (over x), tp: 32 (over z, y, core).
Axes of the slice: x: 4, y: 4, z: 4, core: 2. Of those that a mesh axis runs over, the one named last changes fastest.
Arguments:
- embeddings: bfloat16 [1536, 393216], P('tp', 'grp')
- counts: int32 [4], replicated, may hold values from 1 to 98304, 294912 in all
Outputs:
- factor: float32 [1536, 1536], P(None, 'tp')
The draws below stay inside these ranges and needn't reach their ends.
Inputs may be any that keep to these rules, and one draw needn't show every extreme that they name: Every group has at least one valid document; the counts sum to 294912 and the largest is 98304.
All inputs are finite; a program needn't handle non-finite values.
Results may differ from the reference program's by a relative error of at most 0.0003.
Values may be sent and summed in bfloat16 or wider, within the bound.
A program may use at most 128 MiB of HBM per device.

```python
import math
import jax
import jax.numpy as jnp
import numpy as np
from jax import lax

H = 1536
DOCS_DEV = 3072
GROUPS = 4
DOCS_GRP = 98304
N_GRP = 4
N_TP = 32


def draw_embeddings(key, part):
    docs = DOCS_DEV * N_TP * N_GRP
    keys = jax.random.split(key, 4)
    centre = jax.random.normal(keys[0], (H, 1), jnp.float32) * 1.5
    spread = jnp.exp(jax.random.uniform(keys[1], (H, 1), jnp.float32, jnp.log(0.5), jnp.log(2.0)))
    noise = jax.random.normal(keys[2], (H, docs), jnp.float32)
    target = jax.random.randint(keys[3], (N_TP * N_GRP,), 0, N_TP)
    feature_block = jnp.arange(H, dtype=jnp.int32) // (H // N_TP)
    doc_block = jnp.arange(docs, dtype=jnp.int32) // DOCS_DEV
    boost = jnp.where(feature_block[:, None] == target[doc_block][None, :], 3.0, 1.0)
    values = centre + spread * noise * boost
    return values.astype(jnp.bfloat16)


def profile(amount, total, limit, skew):
    loads = [(1 << 20) // math.isqrt(grade ** skew) + 1 for grade in range(2, amount + 1)]
    spare, holding = total - limit - (amount - 1), [1] * (amount - 1)
    while spare > 0:
        movable = [i for i in range(amount - 1) if holding[i] < limit]
        mass, remaining = sum([loads[i] for i in movable]), spare
        for i in movable:
            addition = min(limit - holding[i], max(1, remaining * loads[i] // mass), spare)
            holding[i] = holding[i] + addition
            spare = spare - addition
    return np.array([limit] + holding)


def uneven(own_key, amount, total, limit, slope):
    if amount == 2:
        one = jax.random.randint(own_key, (), max(1, total - limit), min(limit, total - 1) + 1)
        return jnp.stack([one, total - one])
    lengths = jnp.asarray(profile(amount, total, limit, slope), jnp.int32)
    couples = (amount - 1) // 2
    giver, sink = lengths[1:1 + 2 * couples:2], lengths[2:2 + 2 * couples:2]
    margin = jnp.minimum(giver - 1, limit - sink)
    moved = jax.random.randint(jax.random.fold_in(own_key, 1), (couples,), 0, 1 << 20) % (margin + 1)
    lengths = lengths.at[1:1 + 2 * couples:2].set(giver - moved).at[2:2 + 2 * couples:2].set(sink + moved)
    return lengths[jax.random.permutation(jax.random.fold_in(own_key, 2), amount)]


def setup_inputs(seed: int = 0) -> dict:
    splits = jax.random.split(jax.random.key(seed), 3)
    embeddings = draw_embeddings(jax.random.fold_in(splits[2], 71), 0)
    counts = uneven(splits[1], GROUPS, 3 * GROUPS * DOCS_GRP // 4, DOCS_GRP, 1).astype(jnp.int32)
    return dict(embeddings=embeddings, counts=counts)


def reference(embeddings, counts):
    docs_grp = DOCS_DEV * N_TP
    index = jnp.arange(embeddings.shape[1], dtype=jnp.int32)
    group = (index // docs_grp).astype(jnp.int32)
    within = (index % docs_grp).astype(jnp.int32)
    valid = within < counts[group]
    masked = jnp.where(valid[None, :], embeddings, jnp.zeros((), embeddings.dtype))
    gram = lax.dot_general(masked.astype(jnp.float32), masked.astype(jnp.float32), (((1,), (1,)), ((), ())), preferred_element_type=jnp.float32)
    colsum = jnp.sum(masked.astype(jnp.float32), axis=1)
    total = jnp.sum(counts).astype(jnp.float32)
    mean = colsum / total
    cov = gram / total - mean[:, None] * mean[None, :]
    lower = jnp.linalg.cholesky(cov)
    return lower.T
```

```python
import functools
import jax
import jax.numpy as jnp
from jax import lax
from jax.experimental import pallas as pl
from jax.experimental.pallas import tpu as pltpu
from jax.sharding import PartitionSpec as P

F32, BF16, I32 = jnp.float32, jnp.bfloat16, jnp.int32
MESH = pl.DeviceIdType.MESH
NTP, FEAT, H, DOCS = 32, 48, 1536, 3072
B, W, SUB = 128, 256, 16
BLOCKS = H // B
TILES = 80
CHUNKS = 6
PIECES = 2
OFFSETS = [(1, 0), (3, 0), (0, 1), (0, 3), (1, 1), (3, 3), (1, 3), (3, 1), (2, 0), (0, 2), (2, 1), (1, 2), (2, 3), (3, 2), (2, 2)]


def tile_of(i, j):
    return 1 + BLOCKS * i - (i * (i - 1)) // 2 + (j - i)


def aligned(i, size, step=None):
    return pl.ds(pl.multiple_of(i * (step or size), step or size), size)


def gram_kernel(counts_ref, x_ref, g_ref, recv, acc, cs, send_sem, recv_sem, own_sem, out_sem):
    cw = DOCS // CHUNKS
    me = lax.axis_index("tp")
    limit = counts_ref[lax.axis_index("grp")]
    bar = pltpu.get_barrier_semaphore()

    def greet(r, _):
        pl.semaphore_signal(bar, inc=1, device_id={"tp": lax.rem(me + r, NTP)}, device_id_type=MESH)
        return 0

    lax.fori_loop(1, NTP, greet, 0)
    pl.semaphore_wait(bar, NTP - 1)
    mine = pl.ds(pl.multiple_of(me * FEAT, 16), FEAT)

    core, y, z = lax.rem(me, 2), lax.rem(me // 2, 4), me // 8
    pw = cw // PIECES

    def send(n, _):
        c, part = n // PIECES, lax.rem(n, PIECES)
        at = pl.ds(pl.multiple_of(part * pw, pw), pw)
        for dz, dy in OFFSETS + [(0, 0)]:
            chip = lax.rem(z + dz, 4) * 4 + lax.rem(y + dy, 4)
            for dc in range(2) if (dz, dy) != (0, 0) else [1]:
                dst = 2 * chip + lax.rem(core + dc, 2)
                pltpu.make_async_remote_copy(
                    x_ref.at[:, pl.ds(pl.multiple_of(dst * DOCS + n * pw, pw), pw)],
                    recv.at[c, mine, at], send_sem, recv_sem.at[c],
                    device_id={"tp": dst}, device_id_type=MESH).start()
        return 0

    lax.fori_loop(0, CHUNKS * PIECES, send, 0)
    for c in range(CHUNKS):
        pltpu.make_async_copy(
            x_ref.at[:, pl.ds(pl.multiple_of(me * DOCS + c * cw, cw), cw)],
            recv.at[c, mine, :], own_sem.at[c]).start()

    def zero(t, _):
        acc[t] = jnp.zeros((B, B), F32)
        return 0

    lax.fori_loop(0, TILES, zero, 0)
    cs[...] = jnp.zeros((16, H), F32)
    for c in range(CHUNKS):
        others = recv.at[c, pl.ds(0, (NTP - 1) * FEAT), :]
        pltpu.make_async_copy(others, others, recv_sem.at[c]).wait()
        pltpu.make_async_copy(recv.at[c, mine, :], recv.at[c, mine, :], own_sem.at[c]).wait()
        doc = me * DOCS + c * cw + lax.broadcasted_iota(I32, (W, cw), 1)

        def row(i, _):
            x = recv[c, aligned(i, W), :]
            xm = jnp.where(doc < limit, x.astype(F32), 0.0).astype(BF16)
            sums = lax.dot_general(jnp.ones((16, cw), BF16), xm, (((1,), (1,)), ((), ())), preferred_element_type=F32)
            cs[:, aligned(i, W)] = cs[:, aligned(i, W)] + sums

            def col(j, _):
                d = lax.dot_general(xm, recv[c, aligned(j, W), :], (((1,), (1,)), ((), ())), preferred_element_type=F32)
                t0, t1 = tile_of(2 * i, 2 * j), tile_of(2 * i + 1, 2 * j)
                acc[t0] = acc[t0] + d[0:B, 0:B]
                acc[t0 + 1] = acc[t0 + 1] + d[0:B, B:]

                @pl.when(j > i)
                def _():
                    acc[t1] = acc[t1] + d[B:, 0:B]

                acc[t1 + 1] = acc[t1 + 1] + d[B:, B:]
                return 0

            lax.fori_loop(i, H // W, col, 0)
            return 0

        lax.fori_loop(0, H // W, row, 0)
    for b in range(BLOCKS):
        acc[0, b:b + 1, :] = cs[0:1, b * B:(b + 1) * B]
    out = pltpu.make_async_copy(acc, g_ref, out_sem)
    out.start()
    sent = recv.at[:, pl.ds(0, (NTP - 1) * FEAT), :]
    pltpu.make_async_copy(sent, sent, send_sem).wait()
    out.wait()


def gram(counts, x):
    any_space = pl.BlockSpec(memory_space=pl.ANY)
    return pl.pallas_call(
        gram_kernel,
        out_shape=jax.ShapeDtypeStruct((TILES, B, B), F32),
        in_specs=[pl.BlockSpec(memory_space=pltpu.SMEM), any_space],
        out_specs=any_space,
        scratch_shapes=[
            pltpu.VMEM((CHUNKS, H, DOCS // CHUNKS), BF16), pltpu.VMEM((TILES, B, B), F32), pltpu.VMEM((16, H), F32),
            pltpu.SemaphoreType.DMA, pltpu.SemaphoreType.DMA((CHUNKS,)), pltpu.SemaphoreType.DMA((CHUNKS,)), pltpu.SemaphoreType.DMA,
        ],
        compiler_params=pltpu.CompilerParams(collective_id=0, has_side_effects=True, vmem_limit_bytes=60 << 20),
        name="gram",
    )(counts, x)


def split(x):
    hi = x.astype(BF16)
    return hi, (x - hi.astype(F32)).astype(BF16)


def factor_block(z_ref):
    for r0 in range(0, B, SUB):
        wd = [jnp.broadcast_to(z_ref[r0 + k:r0 + k + 1, 0:B], (8, B)) for k in range(SUB)]
        wi = [jnp.broadcast_to(z_ref[r0 + k:r0 + k + 1, B:], (8, B)) for k in range(SUB)]
        e = {(k, l): jnp.broadcast_to(wd[k][:, r0 + l:r0 + l + 1], (8, B)) for k in range(SUB) for l in range(k, SUB)}
        for k in range(SUB):
            inv = lax.rsqrt(e[k, k])
            for l in range(k + 1, SUB):
                e[k, l] = e[k, l] * inv
            wd[k] = wd[k] * inv
            wi[k] = wi[k] * inv
            for i in range(k + 1, SUB):
                for l in range(i, SUB):
                    e[i, l] = e[i, l] - e[k, i] * e[k, l]
                wd[i] = wd[i] - e[k, i] * wd[k]
                wi[i] = wi[i] - e[k, i] * wi[k]
            z_ref[r0 + k:r0 + k + 1, 0:B] = wd[k][0:1]
            z_ref[r0 + k:r0 + k + 1, B:] = wi[k][0:1]
        if r0 + SUB < B:
            hi, lo = split(z_ref[r0:r0 + SUB, :])
            left = jnp.concatenate([hi[:, 0:B], hi[:, 0:B], lo[:, 0:B]], axis=0)
            right = jnp.concatenate([hi, lo, hi], axis=0)
            upd = lax.dot_general(left, right, (((0,), (0,)), ((), ())), preferred_element_type=F32)
            z_ref[r0 + SUB:, :] = z_ref[r0 + SUB:, :] - upd[r0 + SUB:, :]


def chol_kernel(counts_ref, g_ref, out_ref, f_ref, a_ref, z_ref, sl_ref, sr_ref, mean_ref, sem):
    load = pltpu.make_async_copy(g_ref, f_ref, sem)
    load.start()
    me = lax.axis_index("tp")
    total = (counts_ref[0] + counts_ref[1] + counts_ref[2] + counts_ref[3]).astype(F32)
    row128 = lax.broadcasted_iota(I32, (B, B), 0)
    col128 = lax.broadcasted_iota(I32, (B, B), 1)

    def clear(i, _):
        a_ref[aligned(i, B), :] = jnp.zeros((B, H), F32)
        return 0

    lax.fori_loop(0, BLOCKS, clear, 0)
    load.wait()
    mean_ref[...] = f_ref[0, 0:16, :] / total

    def panel(p, _):
        rows = aligned(p, B)
        mean_col = jnp.transpose(jnp.broadcast_to(mean_ref[pl.ds(p, 1), :], (B, B)))

        def fill(j, _):
            cov = f_ref[tile_of(p, j)] / total - mean_col * mean_ref[pl.ds(j, 1), :]
            a_ref[rows, aligned(j, B)] = a_ref[rows, aligned(j, B)] + cov
            return 0

        lax.fori_loop(p, BLOCKS, fill, 0)
        z_ref[:, 0:B] = a_ref[rows, rows]
        z_ref[:, B:] = jnp.where(row128 == col128, 1.0, 0.0)
        factor_block(z_ref)
        mhi, mlo = split(z_ref[:, B:])
        mm = jnp.concatenate([mhi, mhi, mlo], axis=1)

        def solve(j, _):
            c = aligned(j, W)
            xhi, xlo = split(a_ref[rows, c])
            r = jnp.dot(mm, jnp.concatenate([xhi, xlo, xhi], axis=0), preferred_element_type=F32)
            a_ref[rows, c] = r
            rhi, rlo = split(r)
            sl_ref[0:B, c] = rhi
            sl_ref[B:2 * B, c] = rhi
            sl_ref[2 * B:, c] = rlo
            sr_ref[0:B, c] = rhi
            sr_ref[B:2 * B, c] = rlo
            sr_ref[2 * B:, c] = rhi
            return 0

        lax.fori_loop(p // 2, H // W, solve, 0)
        a_ref[rows, rows] = jnp.where(row128 <= col128, z_ref[:, 0:B], 0.0)
        sl_ref[:, rows] = jnp.zeros((3 * B, B), BF16)
        sr_ref[:, rows] = jnp.zeros((3 * B, B), BF16)

        def strip(i, _):
            left = sl_ref[:, aligned(i, W)]

            def tile(j, _):
                upd = lax.dot_general(left, sr_ref[:, aligned(j, W)], (((0,), (0,)), ((), ())), preferred_element_type=F32)
                a_ref[aligned(i, W), aligned(j, W)] = a_ref[aligned(i, W), aligned(j, W)] - upd
                return 0

            lax.fori_loop(i, H // W, tile, 0)
            return 0

        lax.fori_loop((p + 1) // 2, H // W, strip, 0)
        return 0

    lax.fori_loop(0, BLOCKS, panel, 0)

    first = me * FEAT
    base = jnp.minimum(first // B, BLOCKS - 2)
    shift = 2 * B - (first - base * B)

    def emit(i, _):
        window = a_ref[aligned(i, B), aligned(base, 2 * B, B)]
        part = pltpu.roll(window, shift, 1)[:, 0:FEAT]
        r = i * B + lax.broadcasted_iota(I32, (B, FEAT), 0)
        c = first + lax.broadcasted_iota(I32, (B, FEAT), 1)
        out_ref[aligned(i, B), :] = jnp.where(r <= c, part, 0.0)
        return 0

    lax.fori_loop(0, BLOCKS, emit, 0)


def chol(counts, g):
    return pl.pallas_call(
        chol_kernel,
        out_shape=jax.ShapeDtypeStruct((H, FEAT), F32),
        in_specs=[pl.BlockSpec(memory_space=pltpu.SMEM), pl.BlockSpec(memory_space=pl.ANY)],
        out_specs=pl.BlockSpec(memory_space=pltpu.VMEM),
        scratch_shapes=[
            pltpu.VMEM((TILES, B, B), F32), pltpu.VMEM((H, H), F32), pltpu.VMEM((B, 2 * B), F32),
            pltpu.VMEM((3 * B, H), BF16), pltpu.VMEM((3 * B, H), BF16), pltpu.VMEM((16, B), F32), pltpu.SemaphoreType.DMA,
        ],
        compiler_params=pltpu.CompilerParams(vmem_limit_bytes=60 << 20),
        name="chol",
    )(counts, g)


def shards(embeddings, counts):
    g = lax.psum(gram(counts, embeddings), ("grp", "tp"))
    return chol(counts, g)


def solution(mesh):
    return jax.shard_map(shards, mesh=mesh, in_specs=(P("tp", "grp"), P()), out_specs=P(None, "tp"), check_vma=False)
```

```python
import functools
import jax
import jax.numpy as jnp
from jax import lax
from jax.experimental import pallas as pl
from jax.experimental.pallas import tpu as pltpu
from jax.sharding import PartitionSpec as P

F32, BF16, I32 = jnp.float32, jnp.bfloat16, jnp.int32
MESH = pl.DeviceIdType.MESH
NTP, FEAT, H, DOCS = 32, 48, 1536, 3072
B, W, SUB = 128, 256, 16
BLOCKS = H // B
TILES = 80
CHIPS, PARTS = 64, 5
HALF = TILES * B // (2 * PARTS)
ROWS = HALF // CHIPS
SCATTER, GATHER, FORWARD, FINISH = range(4)
BEFORE = [(SCATTER, 0), (SCATTER, 1), (GATHER, 0), (SCATTER, 2), (FORWARD, 0), (FINISH, 0)]
DURING = {
    (0, 0): [(GATHER, 1), (SCATTER, 3)], (0, 1): [(FORWARD, 1), (GATHER, 2), (SCATTER, 4), (FINISH, 1)],
    (1, 0): [(FORWARD, 2), (GATHER, 3)], (1, 1): [(FINISH, 2)],
    (2, 0): [(FORWARD, 3), (GATHER, 4)], (2, 1): [(FINISH, 3)],
    (3, 0): [(FORWARD, 4)], (3, 1): [(FINISH, 4)],
}
CHUNKS = 6
PIECES = 2
OFFSETS = [(1, 0), (3, 0), (0, 1), (0, 3), (1, 1), (3, 3), (1, 3), (3, 1), (2, 0), (0, 2), (2, 1), (1, 2), (2, 3), (3, 2), (2, 2)]


def tile_of(i, j):
    return 1 + BLOCKS * i - (i * (i - 1)) // 2 + (j - i)


def aligned(i, size, step=None):
    return pl.ds(pl.multiple_of(i * (step or size), step or size), size)


def gram_kernel(counts_ref, x_ref, g_ref, recv, acc, cs, send_sem, recv_sem, own_sem, out_sem):
    cw = DOCS // CHUNKS
    me = lax.axis_index("tp")
    limit = counts_ref[lax.axis_index("grp")]
    bar = pltpu.get_barrier_semaphore()

    def greet(r, _):
        pl.semaphore_signal(bar, inc=1, device_id={"tp": lax.rem(me + r, NTP)}, device_id_type=MESH)
        return 0

    lax.fori_loop(1, NTP, greet, 0)
    pl.semaphore_wait(bar, NTP - 1)
    mine = pl.ds(pl.multiple_of(me * FEAT, 16), FEAT)

    core, y, z = lax.rem(me, 2), lax.rem(me // 2, 4), me // 8
    pw = cw // PIECES

    def send(n, _):
        c, part = n // PIECES, lax.rem(n, PIECES)
        at = pl.ds(pl.multiple_of(part * pw, pw), pw)
        for dz, dy in OFFSETS + [(0, 0)]:
            chip = lax.rem(z + dz, 4) * 4 + lax.rem(y + dy, 4)
            for dc in range(2) if (dz, dy) != (0, 0) else [1]:
                dst = 2 * chip + lax.rem(core + dc, 2)
                pltpu.make_async_remote_copy(
                    x_ref.at[:, pl.ds(pl.multiple_of(dst * DOCS + n * pw, pw), pw)],
                    recv.at[c, mine, at], send_sem, recv_sem.at[c],
                    device_id={"tp": dst}, device_id_type=MESH).start()
        return 0

    lax.fori_loop(0, CHUNKS * PIECES, send, 0)
    for c in range(CHUNKS):
        pltpu.make_async_copy(
            x_ref.at[:, pl.ds(pl.multiple_of(me * DOCS + c * cw, cw), cw)],
            recv.at[c, mine, :], own_sem.at[c]).start()

    def zero(t, _):
        acc[t] = jnp.zeros((B, B), F32)
        return 0

    lax.fori_loop(0, TILES, zero, 0)
    cs[...] = jnp.zeros((16, H), F32)
    for c in range(CHUNKS):
        others = recv.at[c, pl.ds(0, (NTP - 1) * FEAT), :]
        pltpu.make_async_copy(others, others, recv_sem.at[c]).wait()
        pltpu.make_async_copy(recv.at[c, mine, :], recv.at[c, mine, :], own_sem.at[c]).wait()
        doc = me * DOCS + c * cw + lax.broadcasted_iota(I32, (W, cw), 1)

        def row(i, _):
            x = recv[c, aligned(i, W), :]
            xm = jnp.where(doc < limit, x.astype(F32), 0.0).astype(BF16)
            sums = lax.dot_general(jnp.ones((16, cw), BF16), xm, (((1,), (1,)), ((), ())), preferred_element_type=F32)
            cs[:, aligned(i, W)] = cs[:, aligned(i, W)] + sums

            def col(j, _):
                d = lax.dot_general(xm, recv[c, aligned(j, W), :], (((1,), (1,)), ((), ())), preferred_element_type=F32)
                t0, t1 = tile_of(2 * i, 2 * j), tile_of(2 * i + 1, 2 * j)
                acc[t0] = acc[t0] + d[0:B, 0:B]
                acc[t0 + 1] = acc[t0 + 1] + d[0:B, B:]

                @pl.when(j > i)
                def _():
                    acc[t1] = acc[t1] + d[B:, 0:B]

                acc[t1 + 1] = acc[t1 + 1] + d[B:, B:]
                return 0

            lax.fori_loop(i, H // W, col, 0)
            return 0

        lax.fori_loop(0, H // W, row, 0)
    for b in range(BLOCKS):
        acc[0, b:b + 1, :] = cs[0:1, b * B:(b + 1) * B]
    out = pltpu.make_async_copy(acc, g_ref, out_sem)
    out.start()
    sent = recv.at[:, pl.ds(0, (NTP - 1) * FEAT), :]
    pltpu.make_async_copy(sent, sent, send_sem).wait()
    out.wait()


def gram(counts, x):
    any_space = pl.BlockSpec(memory_space=pl.ANY)
    return pl.pallas_call(
        gram_kernel,
        out_shape=jax.ShapeDtypeStruct((TILES, B, B), F32),
        in_specs=[pl.BlockSpec(memory_space=pltpu.SMEM), any_space],
        out_specs=any_space,
        scratch_shapes=[
            pltpu.VMEM((CHUNKS, H, DOCS // CHUNKS), BF16), pltpu.VMEM((TILES, B, B), F32), pltpu.VMEM((16, H), F32),
            pltpu.SemaphoreType.DMA, pltpu.SemaphoreType.DMA((CHUNKS,)), pltpu.SemaphoreType.DMA((CHUNKS,)), pltpu.SemaphoreType.DMA,
        ],
        compiler_params=pltpu.CompilerParams(collective_id=0, has_side_effects=True, vmem_limit_bytes=60 << 20),
        name="gram",
    )(counts, x)


def split(x):
    hi = x.astype(BF16)
    return hi, (x - hi.astype(F32)).astype(BF16)


def factor_block(z_ref):
    for r0 in range(0, B, SUB):
        wd = [jnp.broadcast_to(z_ref[r0 + k:r0 + k + 1, 0:B], (8, B)) for k in range(SUB)]
        wi = [jnp.broadcast_to(z_ref[r0 + k:r0 + k + 1, B:], (8, B)) for k in range(SUB)]
        e = {(k, l): jnp.broadcast_to(wd[k][:, r0 + l:r0 + l + 1], (8, B)) for k in range(SUB) for l in range(k, SUB)}
        for k in range(SUB):
            inv = lax.rsqrt(e[k, k])
            for l in range(k + 1, SUB):
                e[k, l] = e[k, l] * inv
            wd[k] = wd[k] * inv
            wi[k] = wi[k] * inv
            for i in range(k + 1, SUB):
                for l in range(i, SUB):
                    e[i, l] = e[i, l] - e[k, i] * e[k, l]
                wd[i] = wd[i] - e[k, i] * wd[k]
                wi[i] = wi[i] - e[k, i] * wi[k]
            z_ref[r0 + k:r0 + k + 1, 0:B] = wd[k][0:1]
            z_ref[r0 + k:r0 + k + 1, B:] = wi[k][0:1]
        if r0 + SUB < B:
            hi, lo = split(z_ref[r0:r0 + SUB, :])
            left = jnp.concatenate([hi[:, 0:B], hi[:, 0:B], lo[:, 0:B]], axis=0)
            right = jnp.concatenate([hi, lo, hi], axis=0)
            upd = lax.dot_general(left, right, (((0,), (0,)), ((), ())), preferred_element_type=F32)
            z_ref[r0 + SUB:, :] = z_ref[r0 + SUB:, :] - upd[r0 + SUB:, :]


def chol_kernel(counts_ref, g_ref, out_ref, ex, half, got, f_ref, a_ref, z_ref, sl_ref, sr_ref, mean_ref,
                own_sem, send_sem, ex_sem, rs_sem, ag_sem, sib_sem):
    me, x = lax.axis_index("tp"), lax.axis_index("grp")
    core, y, z = lax.rem(me, 2), lax.rem(me // 2, 4), me // 8
    chip = (x * 4 + z) * 4 + y
    sibling = {"tp": 2 * (me // 2) + 1 - core}

    def peer(r):
        v = lax.rem(r * 27, CHIPS)
        px, pz, py = lax.rem(x + v // 16, 4), lax.rem(z + lax.rem(v // 4, 4), 4), lax.rem(y + lax.rem(v, 4), 4)
        return (px * 4 + pz) * 4 + py, {"grp": px, "tp": (pz * 4 + py) * 2 + core}

    bar = pltpu.get_barrier_semaphore()

    def greet(r, _):
        pl.semaphore_signal(bar, inc=1, device_id=peer(r)[1], device_id_type=MESH)
        return 0

    pl.semaphore_signal(bar, inc=1, device_id=sibling, device_id_type=MESH)
    lax.fori_loop(1, CHIPS, greet, 0)

    def own(q):
        return pltpu.make_async_copy(g_ref.at[2 * q + core], half.at[q], own_sem.at[q])

    for q in range(PARTS):
        own(q).start()

    def clear(i, _):
        a_ref[aligned(i, B), :] = jnp.zeros((B, H), F32)
        return 0

    lax.fori_loop(0, BLOCKS, clear, 0)
    pl.semaphore_wait(bar, CHIPS)
    for q in range(PARTS):
        pltpu.make_async_remote_copy(
            g_ref.at[2 * q + 1 - core], ex.at[q], send_sem, ex_sem.at[q], device_id=sibling, device_id_type=MESH).start()
    piece = aligned(chip, ROWS)

    def scatter(q):
        pltpu.make_async_copy(ex.at[q], ex.at[q], ex_sem.at[q]).wait()
        own(q).wait()

        def add(i, _):
            half[q, aligned(i, B), :] = half[q, aligned(i, B), :] + ex[q, aligned(i, B), :]
            return 0

        lax.fori_loop(0, CHIPS * ROWS // B, add, 0)
        got[q, chip] = half[q, piece, :]

        def send(r, _):
            other, device = peer(r)
            pltpu.make_async_remote_copy(
                half.at[q, aligned(other, ROWS)], got.at[q, chip], send_sem, rs_sem.at[q], device_id=device, device_id_type=MESH).start()
            return 0

        lax.fori_loop(1, CHIPS, send, 0)

    def gather(q):
        others = got.at[q, pl.ds(0, CHIPS - 1)]
        pltpu.make_async_copy(others, others, rs_sem.at[q]).wait()

        f_ref[2 * q + core, piece, :] = jnp.sum(got[q], axis=0)

        def send(r, _):
            at = f_ref.at[2 * q + core, piece]
            pltpu.make_async_remote_copy(at, at, send_sem, ag_sem.at[q], device_id=peer(r)[1], device_id_type=MESH).start()
            return 0

        lax.fori_loop(1, CHIPS, send, 0)

    def forward(q):
        others = f_ref.at[2 * q + core, pl.ds(0, (CHIPS - 1) * ROWS)]
        pltpu.make_async_copy(others, others, ag_sem.at[q]).wait()
        at = f_ref.at[2 * q + core]
        pltpu.make_async_remote_copy(at, at, send_sem, sib_sem.at[q], device_id=sibling, device_id_type=MESH).start()

    def finish(q):
        at = f_ref.at[2 * q + 1 - core]
        pltpu.make_async_copy(at, at, sib_sem.at[q]).wait()

    total = (counts_ref[0] + counts_ref[1] + counts_ref[2] + counts_ref[3]).astype(F32)
    row128 = lax.broadcasted_iota(I32, (B, B), 0)
    col128 = lax.broadcasted_iota(I32, (B, B), 1)

    for step, q in BEFORE:
        (scatter, gather, forward, finish)[step](q)
    mean_ref[...] = f_ref[0, 0:16, :] / total

    def during(p, where):
        for at, steps in DURING.items():
            if at[1] == where:
                @pl.when(p == at[0])
                def _():
                    for step, q in steps:
                        (scatter, gather, forward, finish)[step](q)

    def panel(p, _):
        rows = aligned(p, B)
        mean_col = jnp.transpose(jnp.broadcast_to(mean_ref[pl.ds(p, 1), :], (B, B)))

        def fill(j, _):
            t = tile_of(p, j)
            cov = f_ref[t // 8, aligned(lax.rem(t, 8), B), :] / total - mean_col * mean_ref[pl.ds(j, 1), :]
            a_ref[rows, aligned(j, B)] = a_ref[rows, aligned(j, B)] + cov
            return 0

        lax.fori_loop(p, BLOCKS, fill, 0)
        z_ref[:, 0:B] = a_ref[rows, rows]
        z_ref[:, B:] = jnp.where(row128 == col128, 1.0, 0.0)
        factor_block(z_ref)
        during(p, 0)
        mhi, mlo = split(z_ref[:, B:])
        mm = jnp.concatenate([mhi, mhi, mlo], axis=1)

        def solve(j, _):
            c = aligned(j, W)
            xhi, xlo = split(a_ref[rows, c])
            r = jnp.dot(mm, jnp.concatenate([xhi, xlo, xhi], axis=0), preferred_element_type=F32)
            a_ref[rows, c] = r
            rhi, rlo = split(r)
            sl_ref[0:B, c] = rhi
            sl_ref[B:2 * B, c] = rhi
            sl_ref[2 * B:, c] = rlo
            sr_ref[0:B, c] = rhi
            sr_ref[B:2 * B, c] = rlo
            sr_ref[2 * B:, c] = rhi
            return 0

        lax.fori_loop(p // 2, H // W, solve, 0)
        a_ref[rows, rows] = jnp.where(row128 <= col128, z_ref[:, 0:B], 0.0)
        sl_ref[:, rows] = jnp.zeros((3 * B, B), BF16)
        sr_ref[:, rows] = jnp.zeros((3 * B, B), BF16)

        def strip(i, _):
            left = sl_ref[:, aligned(i, W)]

            def tile(j, _):
                upd = lax.dot_general(left, sr_ref[:, aligned(j, W)], (((0,), (0,)), ((), ())), preferred_element_type=F32)
                a_ref[aligned(i, W), aligned(j, W)] = a_ref[aligned(i, W), aligned(j, W)] - upd
                return 0

            lax.fori_loop(i, H // W, tile, 0)
            return 0

        lax.fori_loop((p + 1) // 2, H // W, strip, 0)
        during(p, 1)
        return 0

    lax.fori_loop(0, BLOCKS, panel, 0)

    first = me * FEAT
    base = jnp.minimum(first // B, BLOCKS - 2)
    shift = 2 * B - (first - base * B)

    def emit(i, _):
        window = a_ref[aligned(i, B), aligned(base, 2 * B, B)]
        part = pltpu.roll(window, shift, 1)[:, 0:FEAT]
        r = i * B + lax.broadcasted_iota(I32, (B, FEAT), 0)
        c = first + lax.broadcasted_iota(I32, (B, FEAT), 1)
        out_ref[aligned(i, B), :] = jnp.where(r <= c, part, 0.0)
        return 0

    lax.fori_loop(0, BLOCKS, emit, 0)
    for sent in (ex, f_ref.at[pl.ds(0, PARTS)]):
        pltpu.make_async_copy(sent, sent, send_sem).wait()
    for buf in (half, f_ref.at[pl.ds(0, PARTS)]):
        others = buf.at[:, pl.ds(0, (CHIPS - 1) * ROWS)]
        pltpu.make_async_copy(others, others, send_sem).wait()


def chol(counts, g):
    return pl.pallas_call(
        chol_kernel,
        out_shape=jax.ShapeDtypeStruct((H, FEAT), F32),
        in_specs=[pl.BlockSpec(memory_space=pltpu.SMEM), pl.BlockSpec(memory_space=pl.ANY)],
        out_specs=pl.BlockSpec(memory_space=pltpu.VMEM),
        scratch_shapes=[
            pltpu.VMEM((PARTS, HALF, B), F32), pltpu.VMEM((PARTS, HALF, B), F32), pltpu.VMEM((PARTS, CHIPS, ROWS, B), F32),
            pltpu.VMEM((2 * PARTS, HALF, B), F32), pltpu.VMEM((H, H), F32), pltpu.VMEM((B, 2 * B), F32),
            pltpu.VMEM((3 * B, H), BF16), pltpu.VMEM((3 * B, H), BF16), pltpu.VMEM((16, B), F32),
            pltpu.SemaphoreType.DMA((PARTS,)), pltpu.SemaphoreType.DMA, pltpu.SemaphoreType.DMA((PARTS,)),
            pltpu.SemaphoreType.DMA((PARTS,)), pltpu.SemaphoreType.DMA((PARTS,)), pltpu.SemaphoreType.DMA((PARTS,)),
        ],
        compiler_params=pltpu.CompilerParams(collective_id=1, has_side_effects=True, vmem_limit_bytes=60 << 20),
        name="chol",
    )(counts, g)


def shards(embeddings, counts):
    return chol(counts, gram(counts, embeddings).reshape(2 * PARTS, HALF, B))


def solution(mesh):
    return jax.shard_map(shards, mesh=mesh, in_specs=(P("tp", "grp"), P()), out_specs=P(None, "tp"), check_vma=False)
```

```python
import jax
import jax.numpy as jnp
from jax import lax
from jax.experimental import pallas as pl
from jax.experimental.pallas import tpu as pltpu
from jax.sharding import PartitionSpec as P

F32, BF16, I32 = jnp.float32, jnp.bfloat16, jnp.int32
MESH = pl.DeviceIdType.MESH
NTP, FEAT, H, DOCS = 32, 48, 1536, 3072
B, W, SUB = 128, 256, 16
BLOCKS, WIDE = H // B, H // W
TILES = 80
CHUNKS = 6
PIECES = 2
OFFSETS = [(1, 0), (3, 0), (0, 1), (0, 3), (1, 1), (3, 3), (1, 3), (3, 1), (2, 0), (0, 2), (2, 1), (1, 2), (2, 3), (3, 2), (2, 2)]
CHIPS = 64
PARTS = [8, 8, 16, 16, 16, 16]
SWAP, SCATTER, GATHER, FORWARD, FINISH = range(5)
LAST = {
    0: [(SWAP, 0), (SWAP, 1)], 1: [(SWAP, 2)], 2: [(SWAP, 3), (SCATTER, 0)], 3: [(SWAP, 4), (SCATTER, 1)],
    5: [(SWAP, 5), (GATHER, 0), (SCATTER, 2), (FORWARD, 0), (GATHER, 1), (FINISH, 0)],
}
DURING = {
    (0, 0): [(FORWARD, 1), (SCATTER, 3), (FINISH, 1)], (0, 1): [(GATHER, 2), (SCATTER, 4), (FORWARD, 2), (GATHER, 3)],
    (1, 0): [(FINISH, 2), (SCATTER, 5), (FORWARD, 3)], (1, 1): [(GATHER, 4)],
    (2, 0): [(FINISH, 3), (FORWARD, 4)], (2, 1): [(GATHER, 5)],
    (3, 0): [(FINISH, 4), (FORWARD, 5)], (4, 0): [(FINISH, 5)],
}


def tile_of(i, j):
    return 1 + BLOCKS * i - (i * (i - 1)) // 2 + (j - i)


def aligned(i, size, step=None):
    return pl.ds(pl.multiple_of(i * (step or size), step or size), size)


def part(q):
    return sum(PARTS[:q]), PARTS[q] * B // 2, PARTS[q] * B // 2 // CHIPS


def split(x):
    hi = x.astype(BF16)
    return hi, (x - hi.astype(F32)).astype(BF16)


def dot_tn(a, b):
    return lax.dot_general(a, b, (((0,), (0,)), ((), ())), preferred_element_type=F32)


def dot_nt(a, b):
    return lax.dot_general(a, b, (((1,), (1,)), ((), ())), preferred_element_type=F32)


def factor_block(z_ref, t_ref, deferred):
    for s in range(B // SUB):
        r0, n0 = s * SUB, (s + 1) * SUB
        last = n0 == B
        if 1 <= s <= WIDE:
            deferred(s - 1)
        for l in range(SUB):
            t_ref[l * SUB:(l + 1) * SUB, :] = jnp.broadcast_to(z_ref[r0:n0, r0 + l:r0 + l + 1], (SUB, B))
        e = {(k, l): jnp.broadcast_to(t_ref[l * SUB + k:l * SUB + k + 1, :], (8, B)) for k in range(SUB) for l in range(k, SUB)}
        wd = [jnp.broadcast_to(z_ref[r0 + k:r0 + k + 1, 0:B], (8, B)) for k in range(SUB)]
        wi = [jnp.broadcast_to(z_ref[r0 + k:r0 + k + 1, B:], (8, B)) for k in range(SUB)]
        if not last:
            zt = jnp.transpose(z_ref[r0:n0, 0:B])
            cc = [[jnp.broadcast_to(zt[n0 + h:n0 + h + 8, k:k + 1], (8, B)) for h in (0, 8)] for k in range(SUB)]
            nxt = [[z_ref[n0 + h:n0 + h + 8, m:m + B] for m in (0, B)] for h in (0, 8)]
        for k in range(SUB):
            inv = lax.rsqrt(e[k, k])
            for l in range(k + 1, SUB):
                e[k, l] = e[k, l] * inv
            wd[k] = wd[k] * inv
            wi[k] = wi[k] * inv
            if not last:
                cc[k] = [c * inv for c in cc[k]]
            for i in range(k + 1, SUB):
                for l in range(i, SUB):
                    e[i, l] = e[i, l] - e[k, i] * e[k, l]
                wd[i] = wd[i] - e[k, i] * wd[k]
                wi[i] = wi[i] - e[k, i] * wi[k]
                if not last:
                    cc[i] = [c - e[k, i] * d for c, d in zip(cc[i], cc[k])]
            if not last:
                nxt = [[v - c * w for v, w in zip(n, (wd[k], wi[k]))] for n, c in zip(nxt, cc[k])]
            z_ref[r0 + k:r0 + k + 1, 0:B] = wd[k][0:1]
            z_ref[r0 + k:r0 + k + 1, B:] = wi[k][0:1]
        if not last:
            for h in range(2):
                for m in range(2):
                    z_ref[n0 + 8 * h:n0 + 8 * h + 8, m * B:(m + 1) * B] = nxt[h][m]
        if n0 + SUB < B:
            hi, lo = split(z_ref[r0:n0, :])
            left = jnp.concatenate([hi[:, 0:B], hi[:, 0:B], lo[:, 0:B]], axis=0)
            upd = dot_tn(left, jnp.concatenate([hi, lo, hi], axis=0))
            z_ref[n0 + SUB:, :] = z_ref[n0 + SUB:, :] - upd[n0 + SUB:, :]


def kernel(counts_ref, x_ref, out_ref, recv, acc, cs, ex, got, f_ref, a_ref, z_ref, t_ref, sl_ref, sr_ref, mean_ref,
           send_sem, recv_sem, own_sem, sum_sem, ex_sem, rs_sem, ag_sem, sib_sem):
    cw = DOCS // CHUNKS
    me, x = lax.axis_index("tp"), lax.axis_index("grp")
    core, y, z = lax.rem(me, 2), lax.rem(me // 2, 4), me // 8
    chip = (x * 4 + z) * 4 + y
    limit = counts_ref[x]
    total = (counts_ref[0] + counts_ref[1] + counts_ref[2] + counts_ref[3]).astype(F32)
    sibling = {"tp": 2 * (me // 2) + 1 - core}

    def peer(r):
        v = lax.rem(r * 27, CHIPS)
        px, pz, py = lax.rem(x + v // 16, 4), lax.rem(z + lax.rem(v // 4, 4), 4), lax.rem(y + lax.rem(v, 4), 4)
        return (px * 4 + pz) * 4 + py, {"grp": px, "tp": (pz * 4 + py) * 2 + core}

    bar = pltpu.get_barrier_semaphore()

    def greet(r, _):
        pl.semaphore_signal(bar, inc=1, device_id={"tp": lax.rem(me + r, NTP)}, device_id_type=MESH)
        return 0

    def greet_far(r, _):
        there = {"grp": lax.rem(x + r // 16, 4), "tp": lax.rem(r, 16) * 2 + core}
        pl.semaphore_signal(bar, inc=1, device_id=there, device_id_type=MESH)
        return 0

    lax.fori_loop(1, NTP, greet, 0)
    lax.fori_loop(16, CHIPS, greet_far, 0)
    pl.semaphore_wait(bar, NTP - 1 + CHIPS - 16)

    mine = pl.ds(pl.multiple_of(me * FEAT, 16), FEAT)
    pw = cw // PIECES

    def send_docs(n, _):
        c, at = n // PIECES, aligned(lax.rem(n, PIECES), pw)
        for dz, dy in OFFSETS + [(0, 0)]:
            there = lax.rem(z + dz, 4) * 4 + lax.rem(y + dy, 4)
            for dc in range(2) if (dz, dy) != (0, 0) else [1]:
                dst = 2 * there + lax.rem(core + dc, 2)
                pltpu.make_async_remote_copy(
                    x_ref.at[:, pl.ds(pl.multiple_of(dst * DOCS + n * pw, pw), pw)],
                    recv.at[c, mine, at], send_sem, recv_sem.at[c],
                    device_id={"tp": dst}, device_id_type=MESH).start()
        return 0

    lax.fori_loop(0, CHUNKS * PIECES, send_docs, 0)
    for c in range(CHUNKS):
        pltpu.make_async_copy(
            x_ref.at[:, pl.ds(pl.multiple_of(me * DOCS + c * cw, cw), cw)],
            recv.at[c, mine, :], own_sem.at[c]).start()

    def clear(i, _):
        a_ref[aligned(i, B), :] = jnp.zeros((B, H), F32)
        return 0

    def clear_tile(t, _):
        acc[aligned(t, B), :] = jnp.zeros((B, B), F32)
        return 0

    lax.fori_loop(0, BLOCKS, clear, 0)
    lax.fori_loop(0, TILES, clear_tile, 0)
    cs[...] = jnp.zeros((16, H), F32)
    for i in range(BLOCKS):
        sl_ref[:, i * B:(i + 1) * B] = jnp.zeros((3 * B, B), BF16)
        sr_ref[:, i * B:(i + 1) * B] = jnp.zeros((3 * B, B), BF16)

    def swap(q):
        t0, half, _ = part(q)
        pltpu.make_async_remote_copy(
            acc.at[pl.ds(pl.multiple_of(t0 * B + (1 - core) * half, half), half), :],
            ex.at[pl.ds(t0 * B // 2, half), :], sum_sem, ex_sem.at[q], device_id=sibling, device_id_type=MESH).start()

    def scatter(q):
        t0, half, rows = part(q)
        e0, h0 = t0 * B // 2, t0 * B + core * half
        theirs = ex.at[pl.ds(e0, half), :]
        pltpu.make_async_copy(theirs, theirs, ex_sem.at[q]).wait()

        def add(i, _):
            at = pl.ds(pl.multiple_of(h0 + i * B, B), B)
            acc[at, :] = acc[at, :] + ex[pl.ds(pl.multiple_of(e0 + i * B, B), B), :]
            return 0

        lax.fori_loop(0, half // B, add, 0)
        slot = pl.ds(pl.multiple_of(e0 + chip * rows, rows), rows)
        got[slot, :] = acc[pl.ds(pl.multiple_of(h0 + chip * rows, rows), rows), :]

        def send(r, _):
            other, device = peer(r)
            pltpu.make_async_remote_copy(
                acc.at[pl.ds(pl.multiple_of(h0 + other * rows, rows), rows), :], got.at[slot, :],
                sum_sem, rs_sem.at[q], device_id=device, device_id_type=MESH).start()
            return 0

        lax.fori_loop(1, CHIPS, send, 0)

    def gather(q):
        t0, half, rows = part(q)
        e0 = t0 * B // 2
        others = got.at[pl.ds(e0, (CHIPS - 1) * rows), :]
        pltpu.make_async_copy(others, others, rs_sem.at[q]).wait()
        at = pl.ds(pl.multiple_of(t0 * B + core * half + chip * rows, rows), rows)
        f_ref[at, :] = jnp.sum(got[e0:e0 + half, :].reshape(CHIPS, rows, B), axis=0)

        def send(r, _):
            pltpu.make_async_remote_copy(
                f_ref.at[at, :], f_ref.at[at, :], sum_sem, ag_sem.at[q], device_id=peer(r)[1], device_id_type=MESH).start()
            return 0

        lax.fori_loop(1, CHIPS, send, 0)

    def forward(q):
        t0, half, rows = part(q)
        h0 = pl.multiple_of(t0 * B + core * half, half)
        others = f_ref.at[pl.ds(h0, (CHIPS - 1) * rows), :]
        pltpu.make_async_copy(others, others, ag_sem.at[q]).wait()
        at = f_ref.at[pl.ds(h0, half), :]
        pltpu.make_async_remote_copy(at, at, sum_sem, sib_sem.at[q], device_id=sibling, device_id_type=MESH).start()

    def finish(q):
        t0, half, _ = part(q)
        at = f_ref.at[pl.ds(pl.multiple_of(t0 * B + (1 - core) * half, half), half), :]
        pltpu.make_async_copy(at, at, sib_sem.at[q]).wait()

    def run(steps):
        for step, q in steps:
            (swap, scatter, gather, forward, finish)[step](q)

    for c in range(CHUNKS):
        others = recv.at[c, pl.ds(0, (NTP - 1) * FEAT), :]
        pltpu.make_async_copy(others, others, recv_sem.at[c]).wait()
        pltpu.make_async_copy(recv.at[c, mine, :], recv.at[c, mine, :], own_sem.at[c]).wait()
        first = me * DOCS + c * cw
        valid = jnp.where(first + lax.broadcasted_iota(I32, (16, cw), 1) < limit, 1.0, 0.0).astype(BF16)

        def sums(i, _):
            cs[:, aligned(i, W)] = cs[:, aligned(i, W)] + dot_nt(valid, recv[c, aligned(i, W), :])
            return 0

        lax.fori_loop(0, WIDE, sums, 0)
        if c == CHUNKS - 1:
            for b in range(BLOCKS):
                acc[b:b + 1, :] = cs[0:1, b * B:(b + 1) * B]

        def row(i, _):
            xm = jnp.where(first + lax.broadcasted_iota(I32, (W, cw), 1) < limit, recv[c, aligned(i, W), :].astype(F32), 0.0).astype(BF16)

            def col(j, _):
                d = dot_nt(xm, recv[c, aligned(j, W), :])
                t0, t1 = tile_of(2 * i, 2 * j), tile_of(2 * i + 1, 2 * j)
                acc[aligned(t0, B), :] = acc[aligned(t0, B), :] + d[0:B, 0:B]
                acc[aligned(t0 + 1, B), :] = acc[aligned(t0 + 1, B), :] + d[0:B, B:]

                @pl.when(j > i)
                def _():
                    acc[aligned(t1, B), :] = acc[aligned(t1, B), :] + d[B:, 0:B]

                acc[aligned(t1 + 1, B), :] = acc[aligned(t1 + 1, B), :] + d[B:, B:]
                return 0

            lax.fori_loop(i, WIDE, col, 0)
            return 0

        if c < CHUNKS - 1:
            lax.fori_loop(0, WIDE, row, 0)
        else:
            for i in range(WIDE):
                row(i, 0)
                run(LAST.get(i, []))

    row128 = lax.broadcasted_iota(I32, (B, B), 0)
    col128 = lax.broadcasted_iota(I32, (B, B), 1)
    mean_ref[...] = f_ref[0:16, :] / total
    column = me * FEAT
    base = jnp.minimum(column // B, BLOCKS - 2)
    shift = 2 * B - (column - base * B)

    def emit(i):
        window = a_ref[aligned(i, B), aligned(base, 2 * B, B)]
        r = i * B + lax.broadcasted_iota(I32, (B, FEAT), 0)
        c = column + lax.broadcasted_iota(I32, (B, FEAT), 1)
        out_ref[aligned(i, B), :] = jnp.where(r <= c, pltpu.roll(window, shift, 1)[:, 0:FEAT], 0.0)

    def during(p, where):
        for (panel_of, place), steps in DURING.items():
            if place == where:
                @pl.when(p == panel_of)
                def _():
                    run(steps)

    def panel(p, _):
        rows = aligned(p, B)
        mean_col = jnp.transpose(jnp.broadcast_to(mean_ref[pl.ds(p, 1), :], (B, B)))

        def cov(j):
            return f_ref[aligned(tile_of(p, j), B), :] / total - mean_col * mean_ref[pl.ds(j, 1), :]

        def deferred(i):
            left = sl_ref[:, i * W:(i + 1) * W]
            for j in range(i, WIDE):
                r, c = slice(i * W, (i + 1) * W), slice(j * W, (j + 1) * W)
                a_ref[r, c] = a_ref[r, c] - dot_tn(left, sr_ref[:, c])

        z_ref[:, 0:B] = a_ref[rows, rows] + cov(p)
        z_ref[:, B:] = jnp.where(row128 == col128, 1.0, 0.0)
        emit(jnp.maximum(p - 1, 0))
        factor_block(z_ref, t_ref, deferred)
        during(p, 0)

        def fill(j, _):
            a_ref[rows, aligned(j, B)] = a_ref[rows, aligned(j, B)] + cov(j)
            return 0

        lax.fori_loop(p + 1, BLOCKS, fill, 0)
        mhi, mlo = split(z_ref[:, B:])
        mm = jnp.concatenate([mhi, mhi, mlo], axis=1)
        for j in range(WIDE):
            @pl.when(j >= p // 2)
            def _():
                c = slice(j * W, (j + 1) * W)
                xhi, xlo = split(a_ref[rows, c])
                r = jnp.dot(mm, jnp.concatenate([xhi, xlo, xhi], axis=0), preferred_element_type=F32)
                a_ref[rows, c] = r
                rhi, rlo = split(r)
                sl_ref[0:B, c] = rhi
                sl_ref[B:2 * B, c] = rhi
                sl_ref[2 * B:, c] = rlo
                sr_ref[0:B, c] = rhi
                sr_ref[B:2 * B, c] = rlo
                sr_ref[2 * B:, c] = rhi

        a_ref[rows, rows] = jnp.where(row128 <= col128, z_ref[:, 0:B], 0.0)
        for b in (p, 2 * (p // 2)):
            sl_ref[:, aligned(b, B)] = jnp.zeros((3 * B, B), BF16)
            sr_ref[:, aligned(b, B)] = jnp.zeros((3 * B, B), BF16)

        @pl.when(p + 1 < BLOCKS)
        def _():
            below = aligned(p + 1, B)
            left = sl_ref[:, below]
            for j in range(WIDE):
                c = slice(j * W, (j + 1) * W)
                a_ref[below, c] = a_ref[below, c] - dot_tn(left, sr_ref[:, c])
            sl_ref[:, below] = jnp.zeros((3 * B, B), BF16)

        during(p, 1)
        return 0

    lax.fori_loop(0, BLOCKS, panel, 0)
    emit(BLOCKS - 1)

    sent = recv.at[:, pl.ds(0, (NTP - 1) * FEAT), :]
    pltpu.make_async_copy(sent, sent, send_sem).wait()
    whole, pieces = TILES * B // 2, TILES * B // 2 // CHIPS * (CHIPS - 1)
    for size in (whole, pieces, pieces, whole):
        sent = f_ref.at[pl.ds(0, size), :]
        pltpu.make_async_copy(sent, sent, sum_sem).wait()


def shards(embeddings, counts):
    rows = TILES * B
    n, dma = len(PARTS), pltpu.SemaphoreType.DMA
    return pl.pallas_call(
        kernel,
        out_shape=jax.ShapeDtypeStruct((H, FEAT), F32),
        in_specs=[pl.BlockSpec(memory_space=pltpu.SMEM), pl.BlockSpec(memory_space=pl.ANY)],
        out_specs=pl.BlockSpec(memory_space=pltpu.VMEM),
        scratch_shapes=[
            pltpu.VMEM((CHUNKS, H, DOCS // CHUNKS), BF16), pltpu.VMEM((rows, B), F32), pltpu.VMEM((16, H), F32),
            pltpu.VMEM((rows // 2, B), F32), pltpu.VMEM((rows // 2, B), F32), pltpu.VMEM((rows, B), F32),
            pltpu.VMEM((H, H), F32), pltpu.VMEM((B, 2 * B), F32), pltpu.VMEM((SUB * SUB, B), F32),
            pltpu.VMEM((3 * B, H), BF16), pltpu.VMEM((3 * B, H), BF16), pltpu.VMEM((16, B), F32),
            dma, dma((CHUNKS,)), dma((CHUNKS,)), dma, dma((n,)), dma((n,)), dma((n,)), dma((n,)),
        ],
        compiler_params=pltpu.CompilerParams(collective_id=0, has_side_effects=True, vmem_limit_bytes=60 << 20),
        name="whiten",
    )(counts, embeddings)


def solution(mesh):
    return jax.shard_map(shards, mesh=mesh, in_specs=(P("tp", "grp"), P()), out_specs=P(None, "tp"), check_vma=False)
```

```python
import jax
import jax.numpy as jnp
from jax import lax
from jax.experimental import pallas as pl
from jax.experimental.pallas import tpu as pltpu
from jax.sharding import PartitionSpec as P

F32, BF16, I32 = jnp.float32, jnp.bfloat16, jnp.int32
MESH = pl.DeviceIdType.MESH
NTP, FEAT, H, DOCS = 32, 48, 1536, 3072
B, W, SUB = 128, 256, 16
BLOCKS, WIDE = H // B, H // W
TILES = 80
CHUNKS = 6
PIECES = 2
OFFSETS = [(1, 0), (3, 0), (0, 1), (0, 3), (1, 1), (3, 3), (1, 3), (3, 1), (2, 0), (0, 2), (2, 1), (1, 2), (2, 3), (3, 2), (2, 2)]
CHIPS = 64
PARTS = [8, 8, 16, 16, 16, 16]
AXES = [1, 2, 0, 1, 2, 0]
SWAP, LINE, PLANE, SPREAD, RETURN, FORWARD, FINISH = range(7)
LAST = {
    0: [(SWAP, 0), (SWAP, 1)], 1: [(SWAP, 2)], 2: [(SWAP, 3), (LINE, 0)], 3: [(SWAP, 4), (LINE, 1)],
    5: [(SWAP, 5), (PLANE, 0), (LINE, 2), (PLANE, 1), (SPREAD, 0), (PLANE, 2), (SPREAD, 1), (RETURN, 0), (LINE, 3), (SPREAD, 2),
        (RETURN, 1), (FORWARD, 0), (LINE, 4), (PLANE, 3), (FORWARD, 1), (FINISH, 0)],
}
DURING = {
    (0, 0): [(RETURN, 2), (LINE, 5), (PLANE, 4), (SPREAD, 3), (FINISH, 1)], (0, 1): [(FORWARD, 2), (RETURN, 3)],
    (1, 0): [(FINISH, 2), (FORWARD, 3), (SPREAD, 4), (PLANE, 5)], (1, 1): [(RETURN, 4)],
    (2, 0): [(FINISH, 3), (FORWARD, 4), (SPREAD, 5)], (2, 1): [(RETURN, 5)],
    (3, 0): [(FINISH, 4), (FORWARD, 5)], (4, 0): [(FINISH, 5)],
}

def tile_of(i, j):
    return 1 + BLOCKS * i - (i * (i - 1)) // 2 + (j - i)


def aligned(i, size, step=None):
    return pl.ds(pl.multiple_of(i * (step or size), step or size), size)


def part(q):
    return sum(PARTS[:q]), PARTS[q] * B // 2, PARTS[q] * B // 2 // CHIPS


def split(x):
    hi = x.astype(BF16)
    return hi, (x - hi.astype(F32)).astype(BF16)


def dot_tn(a, b):
    return lax.dot_general(a, b, (((0,), (0,)), ((), ())), preferred_element_type=F32)


def dot_nt(a, b):
    return lax.dot_general(a, b, (((1,), (1,)), ((), ())), preferred_element_type=F32)


def factor_block(z_ref, t_ref, deferred):
    for s in range(B // SUB):
        r0, n0 = s * SUB, (s + 1) * SUB
        last = n0 == B
        if 1 <= s <= WIDE:
            deferred(s - 1)
        for l in range(SUB):
            t_ref[l * SUB:(l + 1) * SUB, :] = jnp.broadcast_to(z_ref[r0:n0, r0 + l:r0 + l + 1], (SUB, B))
        e = {(k, l): jnp.broadcast_to(t_ref[l * SUB + k:l * SUB + k + 1, :], (8, B)) for k in range(SUB) for l in range(k, SUB)}
        wd = [jnp.broadcast_to(z_ref[r0 + k:r0 + k + 1, 0:B], (8, B)) for k in range(SUB)]
        wi = [jnp.broadcast_to(z_ref[r0 + k:r0 + k + 1, B:], (8, B)) for k in range(SUB)]
        if not last:
            zt = jnp.transpose(z_ref[r0:n0, 0:B])
            cc = [[jnp.broadcast_to(zt[n0 + h:n0 + h + 8, k:k + 1], (8, B)) for h in (0, 8)] for k in range(SUB)]
            nxt = [[z_ref[n0 + h:n0 + h + 8, m:m + B] for m in (0, B)] for h in (0, 8)]
        for k in range(SUB):
            inv = lax.rsqrt(e[k, k])
            for l in range(k + 1, SUB):
                e[k, l] = e[k, l] * inv
            wd[k] = wd[k] * inv
            wi[k] = wi[k] * inv
            if not last:
                cc[k] = [c * inv for c in cc[k]]
            for i in range(k + 1, SUB):
                for l in range(i, SUB):
                    e[i, l] = e[i, l] - e[k, i] * e[k, l]
                wd[i] = wd[i] - e[k, i] * wd[k]
                wi[i] = wi[i] - e[k, i] * wi[k]
                if not last:
                    cc[i] = [c - e[k, i] * d for c, d in zip(cc[i], cc[k])]
            if not last:
                nxt = [[v - c * w for v, w in zip(n, (wd[k], wi[k]))] for n, c in zip(nxt, cc[k])]
            z_ref[r0 + k:r0 + k + 1, 0:B] = wd[k][0:1]
            z_ref[r0 + k:r0 + k + 1, B:] = wi[k][0:1]
        if not last:
            for h in range(2):
                for m in range(2):
                    z_ref[n0 + 8 * h:n0 + 8 * h + 8, m * B:(m + 1) * B] = nxt[h][m]
        if n0 + SUB < B:
            hi, lo = split(z_ref[r0:n0, :])
            left = jnp.concatenate([hi[:, 0:B], hi[:, 0:B], lo[:, 0:B]], axis=0)
            upd = dot_tn(left, jnp.concatenate([hi, lo, hi], axis=0))
            z_ref[n0 + SUB:, :] = z_ref[n0 + SUB:, :] - upd[n0 + SUB:, :]


def kernel(counts_ref, x_ref, out_ref, recv, acc, cs, ex, got, lsum, pgot, f_ref, a_ref, z_ref, t_ref, sl_ref, sr_ref, mean_ref,
           send_sem, recv_sem, own_sem, sum_sem, ex_sem, rs_sem, ps_sem, pg_sem, ag_sem, sib_sem):
    cw = DOCS // CHUNKS
    me, x = lax.axis_index("tp"), lax.axis_index("grp")
    core, y, z = lax.rem(me, 2), lax.rem(me // 2, 4), me // 8
    limit = counts_ref[x]
    total = (counts_ref[0] + counts_ref[1] + counts_ref[2] + counts_ref[3]).astype(F32)
    sibling = {"tp": 2 * (me // 2) + 1 - core}

    def line(q):
        at, a = [x, z, y], AXES[q]
        others = []
        for d in (1, 3, 2):
            to = list(at)
            to[a] = lax.rem(at[a] + d, 4)
            others.append((to[a], {"grp": to[0], "tp": (to[1] * 4 + to[2]) * 2 + core}))
        return at[a], others

    def plane(q):
        at, (b, c) = [x, z, y], [n for n in range(3) if n != AXES[q]]
        others = []
        for db, dc in OFFSETS:
            to = list(at)
            to[b], to[c] = lax.rem(at[b] + db, 4), lax.rem(at[c] + dc, 4)
            others.append((to[b] * 4 + to[c], {"grp": to[0], "tp": (to[1] * 4 + to[2]) * 2 + core}))
        return at[b] * 4 + at[c], others

    bar = pltpu.get_barrier_semaphore()

    def greet(r, _):
        pl.semaphore_signal(bar, inc=1, device_id={"tp": lax.rem(me + r, NTP)}, device_id_type=MESH)
        return 0

    def greet_far(r, _):
        there = {"grp": lax.rem(x + r // 16, 4), "tp": lax.rem(r, 16) * 2 + core}
        pl.semaphore_signal(bar, inc=1, device_id=there, device_id_type=MESH)
        return 0

    lax.fori_loop(1, NTP, greet, 0)
    lax.fori_loop(16, CHIPS, greet_far, 0)
    pl.semaphore_wait(bar, NTP - 1 + CHIPS - 16)

    mine = pl.ds(pl.multiple_of(me * FEAT, 16), FEAT)
    pw = cw // PIECES

    def send_docs(n, _):
        c, at = n // PIECES, aligned(lax.rem(n, PIECES), pw)
        for dz, dy in OFFSETS + [(0, 0)]:
            there = lax.rem(z + dz, 4) * 4 + lax.rem(y + dy, 4)
            for dc in range(2) if (dz, dy) != (0, 0) else [1]:
                dst = 2 * there + lax.rem(core + dc, 2)
                pltpu.make_async_remote_copy(
                    x_ref.at[:, pl.ds(pl.multiple_of(dst * DOCS + n * pw, pw), pw)],
                    recv.at[c, mine, at], send_sem, recv_sem.at[c],
                    device_id={"tp": dst}, device_id_type=MESH).start()
        return 0

    lax.fori_loop(0, CHUNKS * PIECES, send_docs, 0)
    for c in range(CHUNKS):
        pltpu.make_async_copy(
            x_ref.at[:, pl.ds(pl.multiple_of(me * DOCS + c * cw, cw), cw)],
            recv.at[c, mine, :], own_sem.at[c]).start()

    def clear(i, _):
        a_ref[aligned(i, B), :] = jnp.zeros((B, H), F32)
        return 0

    def clear_tile(t, _):
        acc[aligned(t, B), :] = jnp.zeros((B, B), F32)
        return 0

    lax.fori_loop(0, BLOCKS, clear, 0)
    lax.fori_loop(0, TILES, clear_tile, 0)
    cs[...] = jnp.zeros((16, H), F32)
    for i in range(BLOCKS):
        sl_ref[:, i * B:(i + 1) * B] = jnp.zeros((3 * B, B), BF16)
        sr_ref[:, i * B:(i + 1) * B] = jnp.zeros((3 * B, B), BF16)

    def swap(q):
        t0, half, _ = part(q)
        pltpu.make_async_remote_copy(
            acc.at[pl.ds(pl.multiple_of(t0 * B + (1 - core) * half, half), half), :],
            ex.at[pl.ds(t0 * B // 2, half), :], sum_sem, ex_sem.at[q], device_id=sibling, device_id_type=MESH).start()

    def rows_at(start, size):
        return pl.ds(pl.multiple_of(start, size), size)

    def push(src, dst, sem, device):
        pltpu.make_async_remote_copy(src, dst, sum_sem, sem, device_id=device, device_id_type=MESH).start()

    def arrived(ref, sem):
        pltpu.make_async_copy(ref, ref, sem).wait()

    def along(q):
        t0, half, rows = part(q)
        e0, h0, quarter = t0 * B // 2, t0 * B + core * half, half // 4
        arrived(ex.at[pl.ds(e0, half), :], ex_sem.at[q])

        def add(i, _):
            at = rows_at(h0 + i * B, B)
            acc[at, :] = acc[at, :] + ex[rows_at(e0 + i * B, B), :]
            return 0

        lax.fori_loop(0, half // B, add, 0)
        place, others = line(q)
        slot = rows_at(e0 + place * quarter, quarter)
        for to, device in others:
            push(acc.at[rows_at(h0 + to * quarter, quarter), :], got.at[slot, :], rs_sem.at[q], device)
        got[slot, :] = acc[rows_at(h0 + place * quarter, quarter), :]

    def across(q):
        t0, half, rows = part(q)
        e0, quarter = t0 * B // 2, half // 4
        arrived(got.at[pl.ds(e0, 3 * quarter), :], rs_sem.at[q])
        p0 = e0 // 4
        lsum[p0:p0 + quarter, :] = jnp.sum(got[e0:e0 + half, :].reshape(4, quarter, B), axis=0)
        place, others = plane(q)
        slot = rows_at(p0 + place * rows, rows)
        for to, device in others:
            push(lsum.at[rows_at(p0 + to * rows, rows), :], pgot.at[slot, :], ps_sem.at[q], device)
        pgot[slot, :] = lsum[slot, :]

    def spread(q):
        t0, half, rows = part(q)
        quarter = half // 4
        p0 = t0 * B // 8
        arrived(pgot.at[pl.ds(p0, 15 * rows), :], ps_sem.at[q])
        place, others = plane(q)
        at = rows_at(t0 * B + core * half + line(q)[0] * quarter + place * rows, rows)
        f_ref[at, :] = jnp.sum(pgot[p0:p0 + quarter, :].reshape(16, rows, B), axis=0)
        for _, device in others:
            push(f_ref.at[at, :], f_ref.at[at, :], pg_sem.at[q], device)

    def back(q):
        t0, half, rows = part(q)
        quarter = half // 4
        place, others = line(q)
        q0 = pl.multiple_of(t0 * B + core * half + place * quarter, quarter)
        arrived(f_ref.at[pl.ds(q0, 15 * rows), :], pg_sem.at[q])
        at = f_ref.at[pl.ds(q0, quarter), :]
        for _, device in others:
            push(at, at, ag_sem.at[q], device)

    def forward(q):
        t0, half, _ = part(q)
        h0 = pl.multiple_of(t0 * B + core * half, half)
        arrived(f_ref.at[pl.ds(h0, 3 * (half // 4)), :], ag_sem.at[q])
        at = f_ref.at[pl.ds(h0, half), :]
        push(at, at, sib_sem.at[q], sibling)

    def finish(q):
        t0, half, _ = part(q)
        at = f_ref.at[pl.ds(pl.multiple_of(t0 * B + (1 - core) * half, half), half), :]
        pltpu.make_async_copy(at, at, sib_sem.at[q]).wait()

    def run(steps):
        for step, q in steps:
            (swap, along, across, spread, back, forward, finish)[step](q)

    for c in range(CHUNKS):
        others = recv.at[c, pl.ds(0, (NTP - 1) * FEAT), :]
        pltpu.make_async_copy(others, others, recv_sem.at[c]).wait()
        pltpu.make_async_copy(recv.at[c, mine, :], recv.at[c, mine, :], own_sem.at[c]).wait()
        first = me * DOCS + c * cw
        valid = jnp.where(first + lax.broadcasted_iota(I32, (16, cw), 1) < limit, 1.0, 0.0).astype(BF16)

        def sums(i, _):
            cs[:, aligned(i, W)] = cs[:, aligned(i, W)] + dot_nt(valid, recv[c, aligned(i, W), :])
            return 0

        lax.fori_loop(0, WIDE, sums, 0)
        if c == CHUNKS - 1:
            for b in range(BLOCKS):
                acc[b:b + 1, :] = cs[0:1, b * B:(b + 1) * B]

        def row(i, _):
            xm = jnp.where(first + lax.broadcasted_iota(I32, (W, cw), 1) < limit, recv[c, aligned(i, W), :].astype(F32), 0.0).astype(BF16)

            def col(j, _):
                d = dot_nt(xm, recv[c, aligned(j, W), :])
                t0, t1 = tile_of(2 * i, 2 * j), tile_of(2 * i + 1, 2 * j)
                acc[aligned(t0, B), :] = acc[aligned(t0, B), :] + d[0:B, 0:B]
                acc[aligned(t0 + 1, B), :] = acc[aligned(t0 + 1, B), :] + d[0:B, B:]

                @pl.when(j > i)
                def _():
                    acc[aligned(t1, B), :] = acc[aligned(t1, B), :] + d[B:, 0:B]

                acc[aligned(t1 + 1, B), :] = acc[aligned(t1 + 1, B), :] + d[B:, B:]
                return 0

            lax.fori_loop(i, WIDE, col, 0)
            return 0

        if c < CHUNKS - 1:
            lax.fori_loop(0, WIDE, row, 0)
        else:
            for i in range(WIDE):
                row(i, 0)
                run(LAST.get(i, []))

    row128 = lax.broadcasted_iota(I32, (B, B), 0)
    col128 = lax.broadcasted_iota(I32, (B, B), 1)
    mean_ref[...] = f_ref[0:16, :] / total
    column = me * FEAT
    base = jnp.minimum(column // B, BLOCKS - 2)
    shift = 2 * B - (column - base * B)

    def emit(i):
        window = a_ref[aligned(i, B), aligned(base, 2 * B, B)]
        r = i * B + lax.broadcasted_iota(I32, (B, FEAT), 0)
        c = column + lax.broadcasted_iota(I32, (B, FEAT), 1)
        out_ref[aligned(i, B), :] = jnp.where(r <= c, pltpu.roll(window, shift, 1)[:, 0:FEAT], 0.0)

    def during(p, where):
        for (panel_of, place), steps in DURING.items():
            if place == where:
                @pl.when(p == panel_of)
                def _():
                    run(steps)

    def panel(p, _):
        rows = aligned(p, B)
        mean_col = jnp.transpose(jnp.broadcast_to(mean_ref[pl.ds(p, 1), :], (B, B)))

        def cov(j):
            return f_ref[aligned(tile_of(p, j), B), :] / total - mean_col * mean_ref[pl.ds(j, 1), :]

        def deferred(i):
            left = sl_ref[:, i * W:(i + 1) * W]
            for j in range(i, WIDE):
                r, c = slice(i * W, (i + 1) * W), slice(j * W, (j + 1) * W)
                a_ref[r, c] = a_ref[r, c] - dot_tn(left, sr_ref[:, c])

        z_ref[:, 0:B] = a_ref[rows, rows] + cov(p)
        z_ref[:, B:] = jnp.where(row128 == col128, 1.0, 0.0)
        emit(jnp.maximum(p - 1, 0))
        factor_block(z_ref, t_ref, deferred)
        during(p, 0)

        def fill(j, _):
            a_ref[rows, aligned(j, B)] = a_ref[rows, aligned(j, B)] + cov(j)
            return 0

        lax.fori_loop(p + 1, BLOCKS, fill, 0)
        mhi, mlo = split(z_ref[:, B:])
        mm = jnp.concatenate([mhi, mhi, mlo], axis=1)
        for j in range(WIDE):
            @pl.when(j >= p // 2)
            def _():
                c = slice(j * W, (j + 1) * W)
                xhi, xlo = split(a_ref[rows, c])
                r = jnp.dot(mm, jnp.concatenate([xhi, xlo, xhi], axis=0), preferred_element_type=F32)
                a_ref[rows, c] = r
                rhi, rlo = split(r)
                sl_ref[0:B, c] = rhi
                sl_ref[B:2 * B, c] = rhi
                sl_ref[2 * B:, c] = rlo
                sr_ref[0:B, c] = rhi
                sr_ref[B:2 * B, c] = rlo
                sr_ref[2 * B:, c] = rhi

        a_ref[rows, rows] = jnp.where(row128 <= col128, z_ref[:, 0:B], 0.0)
        for b in (p, 2 * (p // 2)):
            sl_ref[:, aligned(b, B)] = jnp.zeros((3 * B, B), BF16)
            sr_ref[:, aligned(b, B)] = jnp.zeros((3 * B, B), BF16)

        @pl.when(p + 1 < BLOCKS)
        def _():
            below = aligned(p + 1, B)
            left = sl_ref[:, below]
            for j in range(WIDE):
                c = slice(j * W, (j + 1) * W)
                a_ref[below, c] = a_ref[below, c] - dot_tn(left, sr_ref[:, c])
            sl_ref[:, below] = jnp.zeros((3 * B, B), BF16)

        during(p, 1)
        return 0

    lax.fori_loop(0, BLOCKS, panel, 0)
    emit(BLOCKS - 1)

    sent = recv.at[:, pl.ds(0, (NTP - 1) * FEAT), :]
    pltpu.make_async_copy(sent, sent, send_sem).wait()
    half = TILES * B // 2
    for size in (half, half // 4 * 3, half // 64 * 15, half // 64 * 15, half // 4 * 3, half):
        sent = f_ref.at[pl.ds(0, size), :]
        pltpu.make_async_copy(sent, sent, sum_sem).wait()


def shards(embeddings, counts):
    rows = TILES * B
    n, dma = len(PARTS), pltpu.SemaphoreType.DMA
    return pl.pallas_call(
        kernel,
        out_shape=jax.ShapeDtypeStruct((H, FEAT), F32),
        in_specs=[pl.BlockSpec(memory_space=pltpu.SMEM), pl.BlockSpec(memory_space=pl.ANY)],
        out_specs=pl.BlockSpec(memory_space=pltpu.VMEM),
        scratch_shapes=[
            pltpu.VMEM((CHUNKS, H, DOCS // CHUNKS), BF16), pltpu.VMEM((rows, B), F32), pltpu.VMEM((16, H), F32),
            pltpu.VMEM((rows // 2, B), F32), pltpu.VMEM((rows // 2, B), F32), pltpu.VMEM((rows // 8, B), F32),
            pltpu.VMEM((rows // 8, B), F32), pltpu.VMEM((rows, B), F32),
            pltpu.VMEM((H, H), F32), pltpu.VMEM((B, 2 * B), F32), pltpu.VMEM((SUB * SUB, B), F32),
            pltpu.VMEM((3 * B, H), BF16), pltpu.VMEM((3 * B, H), BF16), pltpu.VMEM((16, B), F32),
            dma, dma((CHUNKS,)), dma((CHUNKS,)), dma, *[dma((n,))] * 6,
        ],
        compiler_params=pltpu.CompilerParams(collective_id=0, has_side_effects=True, vmem_limit_bytes=60 << 20),
        name="whiten",
    )(counts, embeddings)


def solution(mesh):
    return jax.shard_map(shards, mesh=mesh, in_specs=(P("tp", "grp"), P()), out_specs=P(None, "tp"), check_vma=False)
```
